32 devices in a mesh: wide: 8 (over z, x), narrow: 4 (over y, core).
Axes of the slice: x: 2, y: 2, z: 4, core: 2. Of those that a mesh axis runs over, the one named last changes fastest.
Arguments:
- residues: bfloat16 [96, 160, 768], P(('wide', 'narrow')), may hold values from -6 to 6
- chain_lengths: int32 [96], P(('wide', 'narrow')), may hold values from 95 to 160, as said below
- triple_weight: float32 [2, 768, 2304], P(None, ('wide', 'narrow')), may hold values from -0.21875 to 0.21875
- query_bias: float32 [2, 1536], P(None, ('wide', 'narrow')), may hold values from -1.8 to 1.8
- out_weight: float32 [2, 768, 768], P(None, ('wide', 'narrow')), may hold values from -1.5 to 1.5
- out_bias: float32 [2, 768], P(None, ('wide', 'narrow')), may hold values from -1.8 to 1.8
- first_gain: float32 [2, 768], P(None, ('wide', 'narrow')), may hold values from 0.5 to 1.5
- first_shift: float32 [2, 768], P(None, ('wide', 'narrow')), may hold values from -1.8 to 1.8
- expand_weight: float32 [2, 768, 3072], P(None, ('wide', 'narrow')), may hold values from -0.21875 to 0.21875
- expand_bias: float32 [2, 3072], P(None, ('wide', 'narrow')), may hold values from -1.8 to 1.8
- shrink_weight: float32 [2, 3072, 768], P(None, ('wide', 'narrow')), may hold values from -0.109375 to 0.109375
- shrink_bias: float32 [2, 768], P(None, ('wide', 'narrow')), may hold values from -1.8 to 1.8
- second_gain: float32 [2, 768], P(None, ('wide', 'narrow')), may hold values from 0.5 to 1.5
- second_shift: float32 [2, 768], P(None, ('wide', 'narrow')), may hold values from -1.8 to 1.8
- cotangent: bfloat16 [96, 160, 768], P(('wide', 'narrow')), may hold values from -6 to 6
Outputs:
- activations: float32 [96, 160, 768], P(('wide', 'narrow'))
- input_grad: float32 [96, 160, 768], P(('wide', 'narrow'))
- triple_weight_grad: float32 [2, 768, 2304], P(None, ('wide', 'narrow'))
- query_bias_grad: float32 [2, 1536], P(None, ('wide', 'narrow'))
- out_weight_grad: float32 [2, 768, 768], P(None, ('wide', 'narrow'))
- out_bias_grad: float32 [2, 768], P(None, ('wide', 'narrow'))
- first_gain_grad: float32 [2, 768], P(None, ('wide', 'narrow'))
- first_shift_grad: float32 [2, 768], P(None, ('wide', 'narrow'))
- expand_weight_grad: float32 [2, 768, 3072], P(None, ('wide', 'narrow'))
- expand_bias_grad: float32 [2, 3072], P(None, ('wide', 'narrow'))
- shrink_weight_grad: float32 [2, 3072, 768], P(None, ('wide', 'narrow'))
- shrink_bias_grad: float32 [2, 768], P(None, ('wide', 'narrow'))
- second_gain_grad: float32 [2, 768], P(None, ('wide', 'narrow'))
- second_shift_grad: float32 [2, 768], P(None, ('wide', 'narrow'))
The draws below stay inside these ranges and needn't reach their ends.
Inputs may be any that keep to these rules, and one draw needn't show every extreme that they name: `chain_lengths`: true residue counts of the chains; positions at or past a chain's length are padding and are masked as keys.
All inputs are finite; a program needn't handle non-finite values.
Results may differ from the reference program's by a relative error of at most 0.017.
Values may be sent and summed in bfloat16 or wider, within the bound.
No kernel may reach another device: no remote copies, remote signals or barrier semaphores. Data moves between devices by JAX's collectives and lax.ppermute only.
A program may use at most 256 MiB of HBM per device.

```python
import jax
import jax.numpy as jnp
from jax import lax

D = 768
HEADS = 12
HEAD = 64
FF = 3072
LEN = 160
CHAINS_DEV = 3
LAYERS = 2
CHAINS = 96


def draw_chain_lengths(key, part):
    shortest = LEN - LEN * 13 // 32
    drawn = jax.random.randint(key, (CHAINS,), shortest, LEN + 1)
    return drawn.at[0].set(LEN).at[1].set(shortest).astype(jnp.int32)


def steps_of(rng, extent, split, smallest, high):
    level = 1.0
    for dim, shards_of in split:
        heights = jax.random.uniform(jax.random.fold_in(jax.random.fold_in(rng, 6), dim), (shards_of,), jnp.float32, smallest / len(split), high / len(split))
        level = level * jnp.repeat(jnp.exp(heights), extent[dim] // shards_of).reshape((-1,) + (1,) * (len(extent) - 1 - dim))
    return level


def bell_draw(rng, shape, spread, limit, cuts=(), held_as=jnp.bfloat16):
    array = jax.random.normal(rng, shape, jnp.float32) * spread
    if len(cuts) > 0:
        array = steps_of(rng, shape, cuts, -0.22, 0.18) * array
    return jnp.clip(array, min=-limit, max=limit).astype(held_as)


def setup_inputs(seed: int = 0) -> dict:
    splits = jax.random.split(jax.random.key(seed), 16)
    return {
        "residues": bell_draw(splits[0], (CHAINS, LEN, D), 1.0, 6.0, ((0, 32),)),
        "chain_lengths": draw_chain_lengths(jax.random.fold_in(splits[15], 71), 0),
        "triple_weight": bell_draw(splits[2], (LAYERS, D, 3 * D), D ** -0.5, 0.21875, ((1, 32),), jnp.float32),
        "query_bias": bell_draw(splits[3], (LAYERS, 2 * D), 0.3, 1.8, ((1, 32),), jnp.float32),
        "out_weight": bell_draw(splits[4], (LAYERS, D, D), (D // 48) ** -0.5, 1.5, ((1, 32),), jnp.float32),
        "out_bias": bell_draw(splits[5], (LAYERS, D), 0.3, 1.8, ((1, 32),), jnp.float32),
        "first_gain": jnp.clip(1.0 + 0.1 * jax.random.normal(splits[6], (LAYERS, D), jnp.float32), 0.5, 1.5),
        "first_shift": bell_draw(splits[7], (LAYERS, D), 0.3, 1.8, ((1, 32),), jnp.float32),
        "expand_weight": bell_draw(splits[8], (LAYERS, D, FF), D ** -0.5, 0.21875, ((1, 32),), jnp.float32),
        "expand_bias": bell_draw(splits[9], (LAYERS, FF), 0.3, 1.8, ((1, 32),), jnp.float32),
        "shrink_weight": bell_draw(splits[10], (LAYERS, FF, D), FF ** -0.5, 0.109375, ((1, 32),), jnp.float32),
        "shrink_bias": bell_draw(splits[11], (LAYERS, D), 0.3, 1.8, ((1, 32),), jnp.float32),
        "second_gain": jnp.clip(1.0 + 0.1 * jax.random.normal(splits[12], (LAYERS, D), jnp.float32), 0.5, 1.5),
        "second_shift": bell_draw(splits[13], (LAYERS, D), 0.3, 1.8, ((1, 32),), jnp.float32),
        "cotangent": bell_draw(splits[14], (CHAINS, LEN, D), 1.0, 6.0, ((0, 32),)),
    }


@jax.custom_vjp
def low(v):
    return lax.optimization_barrier(v.astype(jnp.bfloat16)).astype(jnp.float32)

@jax.custom_vjp
def low_back(v):
    return v

def low_keep(v):
    return (low(v), None)

def low_pass(kept, grad):
    return (grad,)

def back_keep(v):
    return (v, None)

def back_low(kept, grad):
    return (low(grad),)
low.defvjp(low_keep, low_pass)
low_back.defvjp(back_keep, back_low)
EPS = 1e-06
SCALE = 0.125
precise = lax.Precision.HIGHEST

def normalize(summed, gain, shift):
    average = lax.optimization_barrier(jnp.mean(summed, axis=-1, keepdims=True))
    centered = summed - average
    variance = lax.optimization_barrier(jnp.mean(centered * centered, axis=-1, keepdims=True))
    return centered * lax.rsqrt(variance + EPS) * gain + shift

def attend(pieces):
    query, keys, values, lengths = pieces
    scores = jnp.einsum('cqhe,ckhe->chqk', query, keys, precision=precise) * SCALE
    valid = jnp.arange(LEN)[None, None, None, :] < lengths[:, None, None, None]
    scores = low_back(jnp.where(valid, scores, -1e+30))
    peak = lax.optimization_barrier(jnp.max(scores, axis=-1, keepdims=True))
    expd = jnp.exp(scores - peak)
    probs = expd / lax.optimization_barrier(jnp.sum(expd, axis=-1, keepdims=True))
    weights = low(probs)
    return jnp.einsum('chqk,ckhe->cqhe', weights, values, precision=precise)

def layer(state, params, lengths):
    triple, query_bias, out_weight, out_bias, gain_a, shift_a, expand_weight, expand_bias, shrink_weight, shrink_bias, gain_b, shift_b = [low(piece) for piece in params]
    tokens = state.reshape(CHAINS * LEN, D)
    flat = low(tokens)
    bias = jnp.concatenate([query_bias[:D], jnp.zeros((D,), jnp.float32), query_bias[D:]])
    mixed = low(low_back(jnp.dot(flat, triple, precision=precise) + bias))
    grid = mixed.reshape(CHAINS // CHAINS_DEV, CHAINS_DEV, LEN, 3, HEADS, HEAD)
    groups = lengths.reshape(CHAINS // CHAINS_DEV, CHAINS_DEV)
    attended = lax.map(jax.checkpoint(attend), (grid[:, :, :, 0], grid[:, :, :, 1], grid[:, :, :, 2], groups))
    context = low(low_back(attended.reshape(CHAINS * LEN, D)))
    branch = low_back(jnp.dot(context, out_weight, precision=precise) + out_bias)
    first = normalize(tokens + branch, gain_a, shift_a)
    before = low_back(jnp.dot(low(first), expand_weight, precision=precise) + expand_bias)
    hidden = low(jax.nn.gelu(before, approximate=False))
    shrunk = low_back(jnp.dot(hidden, shrink_weight, precision=precise) + shrink_bias)
    second = normalize(first + shrunk, gain_b, shift_b)
    return second.reshape(CHAINS, LEN, D)

def reference(residues, chain_lengths, triple_weight, query_bias, out_weight, out_bias, first_gain, first_shift, expand_weight, expand_bias, shrink_weight, shrink_bias, second_gain, second_shift, cotangent):
    params = (triple_weight, query_bias, out_weight, out_bias, first_gain, first_shift, expand_weight, expand_bias, shrink_weight, shrink_bias, second_gain, second_shift)

    def forward(start, weights):
        state = start
        for index in range(LAYERS):
            state = layer(state, [piece[index] for piece in weights], chain_lengths)
        return state
    output, pull = jax.vjp(forward, residues.astype(jnp.float32), params)
    grad_start, grads = pull(cotangent.astype(jnp.float32))
    return (output, grad_start, grads[0], grads[1], grads[2], grads[3], grads[4], grads[5], grads[6], grads[7], grads[8], grads[9], grads[10], grads[11])
```

```python
import jax
import jax.numpy as jnp
from jax import lax
from jax.experimental import pallas as pl
from jax.experimental.pallas import tpu as pltpu
from jax.sharding import PartitionSpec as P

HEAD = 64


EPS = 1e-06
SCALE = 0.125


def normalize(summed, gain, shift):
    average = jnp.mean(summed, axis=-1, keepdims=True)
    centered = summed - average
    variance = jnp.mean(centered * centered, axis=-1, keepdims=True)
    return centered * lax.rsqrt(variance + EPS) * gain + shift


def gelu_pair(values):
    cumulative = 0.5 + 0.5 * lax.erf(values * (0.5**0.5))
    density = jnp.exp(values * values * -0.5) * ((2.0 * jnp.pi) ** -0.5)
    return (values * cumulative, cumulative + values * density)


AXES = ("wide", "narrow")
LOW = 8
LANES = 128
SMALL = (1, 3, 4, 5, 7, 9, 10, 11)


def device_index():
    return lax.axis_index("wide") * lax.axis_size("narrow") + lax.axis_index("narrow")


def hop(value, mask, devices):
    return lax.ppermute(value, AXES, [(k, k ^ mask) for k in range(devices)])


class Chain:
    def __init__(self, steps):
        self.steps = steps
        self.pending = list(next(steps))
        self.result = None

    def resume(self, arrived):
        try:
            self.pending = list(self.steps.send(arrived))
        except StopIteration as stop:
            self.pending = []
            self.result = stop.value


def advance(value, *chains):
    chains = [chain for chain in chains if chain.pending]
    pending = [piece for chain in chains for piece in chain.pending]
    value, pending = lax.optimization_barrier((value, pending))
    for chain in chains:
        count = len(chain.pending)
        chain.resume(pending[:count])
        pending = pending[count:]
    return value


def high_masks(devices):
    masks = []
    while LOW << len(masks) < devices:
        masks.append(LOW << len(masks))
    return masks


def gather_steps(pack, split, devices):
    block = pack[None]
    for mask in high_masks(devices):
        (received,) = yield [hop(block, mask, devices)]
        block = jnp.concatenate([block, received], axis=0)
    left, right = block[:, :, :split], block[:, :, split:]
    for mask in (4, 2):
        received = yield [hop(left, mask, devices), hop(right, 6 - mask, devices)]
        left = jnp.concatenate([left, received[0]], axis=0)
        right = jnp.concatenate([right, received[1]], axis=0)
    received = yield [hop(left, 1, devices), hop(right, 1, devices)]
    return (left, received[0], right, received[1])


def assemble(sources, split, columns, devices):
    count, rows = sources[0].shape[:2]
    high = count // 4
    plan = []
    for number, source in enumerate(sources):
        begin = split * (number // 2)
        finish = begin + source.shape[2]
        for output, (first, width, folds) in enumerate(columns):
            for fold in range(folds):
                low = first + fold * width
                a, b = max(low, begin), min(low + width, finish)
                if a < b:
                    plan.append((number, output, fold, a - begin, a - low, b - a))

    def kernel(*refs):
        inputs, outputs, sem = refs[: len(sources)], refs[len(sources) : -1], refs[-1]
        me = device_index()
        for number, output, fold, at, to, width in plan:
            steps = (4, 2) if number < 2 else (2, 4)
            for k in range(count):
                mask = LOW * (k % high) + number % 2
                mask += steps[0] * (k // high % 2) + steps[1] * (k // high // 2)
                pltpu.make_async_copy(
                    inputs[number].at[k, :, pl.ds(at, width)],
                    outputs[output].at[me ^ mask, fold, :, pl.ds(to, width)],
                    sem,
                ).start()
        for out in outputs:
            pltpu.make_async_copy(out, out, sem).wait()

    whole = pl.pallas_call(
        kernel,
        out_shape=[
            jax.ShapeDtypeStruct((devices, folds, rows, width), sources[0].dtype)
            for _, width, folds in columns
        ],
        in_specs=[pl.BlockSpec(memory_space=pl.ANY)] * len(sources),
        out_specs=[pl.BlockSpec(memory_space=pltpu.VMEM)] * len(columns),
        scratch_shapes=[pltpu.SemaphoreType.DMA],
        compiler_params=pltpu.CompilerParams(vmem_limit_bytes=48 * 2**20),
        name="assemble",
    )(*sources)
    return [w.reshape(-1, w.shape[3]) for w in whole]


def as_columns(vector, rows):
    return vector.reshape(-1, rows).T


def pack_small(vectors, rows):
    columns = [
        as_columns(v[index].astype(jnp.bfloat16), rows)
        for index in range(vectors[0].shape[0])
        for v in vectors
    ]
    small = jnp.concatenate(columns, axis=1)
    return jnp.pad(small, ((0, 0), (0, LANES - small.shape[1])))


def unpack_small(whole, vectors, rows):
    table = whole.astype(jnp.float32).T
    devices = table.shape[1] // rows
    found = []
    start = 0
    for index in range(vectors[0].shape[0]):
        layer = []
        for v in vectors:
            count = v.shape[1] // rows
            piece = table[start : start + count]
            if count > 1:
                piece = piece.reshape(count, devices, rows).transpose(1, 0, 2)
            layer.append(piece.reshape(-1))
            start += count
        found.append(layer)
    return found


def pick(value, axis, position):
    return lax.dynamic_index_in_dim(value, position, axis, keepdims=False)


def add_low(left, right):
    total = left.astype(jnp.float32) + right.astype(jnp.float32)
    return total.astype(jnp.bfloat16)


def reduce_steps(left, right, join, devices):
    me = device_index()
    high = devices // LOW
    values = []
    for grad in (left, right):
        rows = grad.shape[0] // devices
        values.append(grad.astype(jnp.bfloat16).reshape(high, 2, 2, 2, rows, grad.shape[1]))
    for masks, axes in (((1, 1), (3, 3)), ((4, 2), (1, 2)), ((2, 4), (1, 1))):
        sides = [(me // mask) % 2 for mask in masks]
        received = yield [
            hop(pick(v, axis, 1 - side), mask, devices)
            for v, axis, side, mask in zip(values, axes, sides, masks)
        ]
        values = [
            add_low(pick(v, axis, side), other)
            for v, axis, side, other in zip(values, axes, sides, received)
        ]
    value = join(*values)
    for mask in reversed(high_masks(devices)):
        value = value.reshape((2, value.shape[0] // 2) + value.shape[1:])
        side = (me // mask) % 2
        (received,) = yield [hop(pick(value, 0, 1 - side), mask, devices)]
        total = pick(value, 0, side).astype(jnp.float32) + received.astype(jnp.float32)
        value = total if mask == LOW else total.astype(jnp.bfloat16)
    return value[0]


def reduce_small_steps(pieces, devices):
    mask = 1
    while mask < devices:
        (received,) = yield [hop(pieces, mask, devices)]
        pieces = pieces + received
        mask *= 2
    return pick(pieces, 0, device_index())


def fold_pair(expand, shrink):
    rows = expand.shape[1]
    width = shrink.shape[2]
    depth = shrink.shape[1] // rows
    parts = [expand[:, :, k * width : (k + 1) * width] for k in range(depth)]
    parts += [shrink[:, k * rows : (k + 1) * rows] for k in range(depth)]
    return jnp.stack(parts, axis=1)


def join_columns(left, right):
    return jnp.concatenate([left, right], axis=2)


def split_heads(mixed, chains):
    grid = mixed.reshape(chains, -1, 3, mixed.shape[1] // (3 * HEAD), HEAD)
    return (grid[:, :, 0], grid[:, :, 1], grid[:, :, 2])


def masked_scores(query, keys, lengths):
    scores = jnp.einsum("cqhe,ckhe->chqk", query, keys, preferred_element_type=jnp.float32) * SCALE
    valid = jnp.arange(keys.shape[1])[None, None, None, :] < lengths[:, None, None, None]
    return jnp.where(valid, scores, -1e30)


def attend_forward(mixed, lengths, chains):
    query, keys, values = split_heads(mixed, chains)
    scores = masked_scores(query, keys, lengths)
    peak = jnp.max(scores, axis=-1, keepdims=True)
    expd = jnp.exp(scores - peak)
    total = jnp.sum(expd, axis=-1, keepdims=True)
    weights = (expd / total).astype(jnp.bfloat16)
    context = jnp.einsum("chqk,ckhe->cqhe", weights, values, preferred_element_type=jnp.float32)
    width = mixed.shape[1] // 3
    return (context.reshape(-1, width).astype(jnp.bfloat16), peak + jnp.log(total))


def attend_backward(mixed, totals, context_grad, lengths, chains):
    query, keys, values = split_heads(mixed, chains)
    scores = masked_scores(query, keys, lengths)
    probs = jnp.exp(scores - totals)
    weights = probs.astype(jnp.bfloat16)
    grad_heads = context_grad.reshape(query.shape)
    value_grad = jnp.einsum(
        "chqk,cqhe->ckhe", weights, grad_heads, preferred_element_type=jnp.float32
    )
    prob_grad = jnp.einsum(
        "cqhe,ckhe->chqk", grad_heads, values, preferred_element_type=jnp.float32
    )
    delta = jnp.sum(probs * prob_grad, axis=-1, keepdims=True)
    score_grad = (probs * (prob_grad - delta)).astype(jnp.bfloat16)
    query_grad = (
        jnp.einsum("chqk,ckhe->cqhe", score_grad, keys, preferred_element_type=jnp.float32) * SCALE
    )
    key_grad = (
        jnp.einsum("chqk,cqhe->ckhe", score_grad, query, preferred_element_type=jnp.float32) * SCALE
    )
    stacked = jnp.stack([query_grad, key_grad, value_grad], axis=2)
    return stacked.reshape(mixed.shape).astype(jnp.bfloat16)


def forward_layer(state, first_half, second_half, vectors, lengths, tick):
    query_bias, out_bias, gain_a, shift_a, expand_bias, shrink_bias, gain_b, shift_b = vectors
    chains, length, width = state.shape
    tokens = state.reshape(chains * length, width)
    flat = tokens.astype(jnp.bfloat16)
    triple, out_weight = first_half()
    bias = jnp.concatenate([query_bias[:width], jnp.zeros((width,), jnp.float32), query_bias[width:]])
    mixed = (jnp.dot(flat, triple, preferred_element_type=jnp.float32) + bias).astype(jnp.bfloat16)
    mixed = tick(mixed, 0)
    context, totals = attend_forward(mixed, lengths, chains)
    context = tick(context, 1)
    branch = jnp.dot(context, out_weight, preferred_element_type=jnp.float32) + out_bias
    summed_a = tokens + branch
    first = normalize(summed_a, gain_a, shift_a)
    first = tick(first, 2)
    expand_weight, shrink_weight = second_half()
    first_low = first.astype(jnp.bfloat16)
    before = jnp.dot(first_low, expand_weight, preferred_element_type=jnp.float32) + expand_bias
    hidden, slope = (piece.astype(jnp.bfloat16) for piece in gelu_pair(before))
    hidden = tick(hidden, 3)
    shrunk = jnp.dot(hidden, shrink_weight, preferred_element_type=jnp.float32) + shrink_bias
    summed_b = first + shrunk
    second = normalize(summed_b, gain_b, shift_b)
    second = tick(second, 4)
    saved = (flat, mixed, totals, context, summed_a, first_low, slope, hidden, summed_b)
    weights = (triple, out_weight, expand_weight, shrink_weight)
    return (second.reshape(chains, length, width), saved, weights)


def backward_layer(grad_state, saved, weights, vectors, lengths, tick, devices):
    triple, out_weight, expand_weight, shrink_weight = weights
    query_bias, out_bias, gain_a, shift_a, expand_bias, shrink_bias, gain_b, shift_b = vectors
    flat, mixed, totals, context, summed_a, first_low, slope, hidden, summed_b = saved
    chains, length, width = grad_state.shape
    grad = grad_state.reshape(chains * length, width)
    _, pull_b = jax.vjp(normalize, summed_b, gain_b, shift_b)
    grad_b, gain_b_grad, shift_b_grad = pull_b(grad)
    shrunk_grad = grad_b.astype(jnp.bfloat16)
    shrink_bias_grad = jnp.sum(shrunk_grad.astype(jnp.float32), axis=0)
    shrink_weight_grad = jnp.einsum(
        "nf,nd->fd", hidden, shrunk_grad, preferred_element_type=jnp.float32
    )
    hidden_grad = jnp.einsum(
        "nd,fd->nf", shrunk_grad, shrink_weight, preferred_element_type=jnp.float32
    )
    before_grad = (slope.astype(jnp.float32) * hidden_grad).astype(jnp.bfloat16)
    expand_bias_grad = jnp.sum(before_grad.astype(jnp.float32), axis=0)
    expand_weight_grad = jnp.einsum(
        "nd,nf->df", first_low, before_grad, preferred_element_type=jnp.float32
    )
    outer = Chain(reduce_steps(expand_weight_grad, shrink_weight_grad, fold_pair, devices))
    before_grad = tick(before_grad, 0, outer)
    first_grad = grad_b + jnp.einsum(
        "nf,df->nd", before_grad, expand_weight, preferred_element_type=jnp.float32
    )
    _, pull_a = jax.vjp(normalize, summed_a, gain_a, shift_a)
    grad_a, gain_a_grad, shift_a_grad = pull_a(first_grad)
    branch_grad = grad_a.astype(jnp.bfloat16)
    out_bias_grad = jnp.sum(branch_grad.astype(jnp.float32), axis=0)
    out_weight_grad = jnp.einsum(
        "nd,ne->de", context, branch_grad, preferred_element_type=jnp.float32
    )
    context_grad = jnp.einsum(
        "ne,de->nd", branch_grad, out_weight, preferred_element_type=jnp.float32
    ).astype(jnp.bfloat16)
    context_grad = tick(context_grad, 1, outer)
    mixed_grad = attend_backward(mixed, totals, context_grad, lengths, chains)
    mixed_grad = tick(mixed_grad, 2, outer)
    column_sums = jnp.sum(mixed_grad.astype(jnp.float32), axis=0)
    query_bias_grad = jnp.concatenate([column_sums[:width], column_sums[2 * width :]])
    triple_grad = jnp.einsum("nd,ne->de", flat, mixed_grad, preferred_element_type=jnp.float32)
    triple_grad = triple_grad.astype(jnp.bfloat16)
    middle = 2 * width
    inner = Chain(
        reduce_steps(
            triple_grad[:, :middle],
            jnp.concatenate([triple_grad[:, middle:], out_weight_grad.astype(jnp.bfloat16)], axis=1),
            join_columns,
            devices,
        )
    )
    tokens_grad = grad_a + jnp.einsum(
        "ne,de->nd", mixed_grad, triple, preferred_element_type=jnp.float32
    )
    tokens_grad = tick(tokens_grad, 3, outer, inner)
    small = (
        query_bias_grad,
        out_bias_grad,
        gain_a_grad,
        shift_a_grad,
        expand_bias_grad,
        shrink_bias_grad,
        gain_b_grad,
        shift_b_grad,
    )
    small = jnp.concatenate([v.reshape(devices, -1) for v in small], axis=1)
    return (tokens_grad.reshape(chains, length, width), outer, inner, small)


def first_pack(shards, index, small):
    parts = [shards[k][index].astype(jnp.bfloat16) for k in (0, 2)]
    return jnp.concatenate(parts + small, axis=1)


def second_pack(shards, index):
    expand, shrink = (shards[k][index].astype(jnp.bfloat16) for k in (6, 8))
    rows = expand.shape[0]
    depth = shrink.shape[0] // rows
    return jnp.concatenate([expand] + [shrink[k * rows : (k + 1) * rows] for k in range(depth)], axis=1)


def body(*shards):
    residues, chain_lengths, *shards, cotangent = shards
    layers, rows, triple_width = shards[0].shape
    width = triple_width // 3
    hidden = shards[6].shape[2]
    depth = hidden // width
    devices = lax.axis_size("wide") * lax.axis_size("narrow")
    vectors = [shards[k] for k in SMALL]
    middle = 2 * width
    inner_columns = [(0, 3 * width, 1), (3 * width, width, 1)]
    outer_columns = [(0, hidden, 1), (hidden, width, depth)]

    chains = []
    previous = None
    for index in range(layers):
        small = [pack_small(vectors, rows)] if index == 0 else []
        for pack, split in (
            (first_pack(shards, index, small), middle + (LANES if small else 0)),
            (second_pack(shards, index), hidden),
        ):
            if previous is not None:
                while len(previous.pending) == 1:
                    pack = advance(pack, previous)
            previous = Chain(gather_steps(pack, split, devices))
            chains.append((previous, split))

    def finish(position, columns, value):
        chain, split = chains[position]
        while chain.pending:
            value = advance(value, chain)
        return assemble(chain.result, split, columns, devices), value

    state = residues.astype(jnp.float32)
    (triple, out_weight, table), state = finish(
        0, inner_columns + [(4 * width, LANES, 1)], state
    )
    small = unpack_small(table, vectors, rows)
    kept = []
    weights = []
    for index in range(layers):
        done = {0: (triple, out_weight)}

        def tick(value, stage):
            at = 2 * index
            if stage < 3:
                value = advance(value, *[c for c, _ in chains[at + 1 : at + 2]])
            else:
                value = advance(value, *[c for c, _ in chains[at + 2 : at + 3]])
            if stage == 2:
                done[1], value = finish(at + 1, outer_columns, value)
            if stage == 4 and index + 1 < layers:
                done[2], value = finish(at + 2, inner_columns, value)
            return value

        state, saved, used = forward_layer(
            state,
            lambda: done[0],
            lambda: done[1],
            small[index],
            chain_lengths,
            tick,
        )
        kept.append(saved)
        weights.append(used)
        if index + 1 < layers:
            triple, out_weight = done[2]
    grad = cotangent.astype(jnp.float32)
    active = []
    reductions = [None] * layers
    smalls = [None] * layers
    for index in reversed(range(layers)):

        def tick(value, stage, *own):
            return advance(value, *own, *active)

        grad, outer, inner, smalls[index] = backward_layer(
            grad, kept[index], weights[index], small[index], chain_lengths, tick, devices
        )
        active += [outer, inner]
        reductions[index] = (outer, inner)
    tail = Chain(reduce_small_steps(jnp.concatenate(smalls, axis=1), devices))
    active.append(tail)
    while any(chain.pending for chain in active):
        grad = advance(grad, *active)
    outputs = [[] for _ in shards]
    start = 0
    for index in range(layers):
        outer, inner = (chain.result for chain in reductions[index])
        outputs[0].append(inner[:, : 3 * width])
        outputs[2].append(inner[:, 3 * width :])
        outputs[6].append(jnp.concatenate(list(outer[:depth]), axis=1))
        outputs[8].append(outer[depth:].reshape(depth * rows, width))
        for k in SMALL:
            size = shards[k].shape[1]
            outputs[k].append(tail.result[start : start + size])
            start += size
    return (state, grad) + tuple(jnp.stack(pieces) for pieces in outputs)


def solution(mesh):
    return jax.shard_map(
        body,
        mesh=mesh,
        in_specs=(
            P(("wide", "narrow"), None, None),
            P(("wide", "narrow")),
            P(None, ("wide", "narrow"), None),
            P(None, ("wide", "narrow")),
            P(None, ("wide", "narrow"), None),
            P(None, ("wide", "narrow")),
            P(None, ("wide", "narrow")),
            P(None, ("wide", "narrow")),
            P(None, ("wide", "narrow"), None),
            P(None, ("wide", "narrow")),
            P(None, ("wide", "narrow"), None),
            P(None, ("wide", "narrow")),
            P(None, ("wide", "narrow")),
            P(None, ("wide", "narrow")),
            P(("wide", "narrow"), None, None),
        ),
        out_specs=(
            P(("wide", "narrow"), None, None),
            P(("wide", "narrow"), None, None),
            P(None, ("wide", "narrow"), None),
            P(None, ("wide", "narrow")),
            P(None, ("wide", "narrow"), None),
            P(None, ("wide", "narrow")),
            P(None, ("wide", "narrow")),
            P(None, ("wide", "narrow")),
            P(None, ("wide", "narrow"), None),
            P(None, ("wide", "narrow")),
            P(None, ("wide", "narrow"), None),
            P(None, ("wide", "narrow")),
            P(None, ("wide", "narrow")),
            P(None, ("wide", "narrow")),
        ),
        check_vma=False,
    )
```
